32 devices in a mesh: hi: 4 (over y, x), lo: 8 (over z, core).
Axes of the slice: x: 2, y: 2, z: 4, core: 2. Of those that a mesh axis runs over, the one named last changes fastest.
Arguments:
- initial_state: float32 [2, 4194304], P(None, ('hi', 'lo')), may hold values from -60 to 60
- gate_angles: float32 [2, 3, 22], replicated, may hold values from -3.140625 to 3.140625
- damp_qubits: int32 [2, 4], replicated, may hold values from 0 to 16, as said below
- kraus_branch: int32 [2, 4], replicated, may hold values 0 or 1
- damping: float32 [2, 4], replicated, may hold values from 0.1 to 0.6
Outputs:
- final_state: float32 [2, 4194304], P(None, ('hi', 'lo'))
- branch_weights: float32 [2, 4], replicated
The draws below stay inside these ranges and needn't reach their ends.
Inputs may be any that keep to these rules, and one draw needn't show every extreme that they name: `damp_qubits`: the 8 entries are distinct qubits.
All inputs are finite; a program needn't handle non-finite values.
Results may differ from the reference program's by a relative error of at most 0.00022.
Values sent between devices are 32-bit elements; how exact they have to be, the bound alone decides.
A program may use at most 128 MiB of HBM per device.

```python
import math
import jax
import jax.numpy as jnp
from jax import lax

AMP_DEV = 131072
LAYERS = 2
KRAUS = 4
AMPS = 4194304
LQ = 17
QUBITS = 22


def draw_initial_state(key, part):
    first_key, second_key = jax.random.split(jax.random.fold_in(key, 17))
    devices = AMPS // AMP_DEV
    positions = lax.iota(jnp.int32, AMPS)
    device_pos = (positions // AMP_DEV).astype(jnp.float32)
    ramp = 2.0 * device_pos / max(devices - 1, 1) - 1.0
    tilts = jax.random.uniform(second_key, (LQ,), jnp.float32, -0.15, 0.15)
    noise = jnp.clip(jax.random.normal(first_key, (2, AMPS), jnp.float32), -5.0, 5.0)
    exponent = jnp.zeros((AMPS,), jnp.float32)
    for qubit_no in range(LQ):
        bit_value = jnp.bitwise_and(jnp.right_shift(positions, qubit_no), 1).astype(jnp.float32)
        exponent = exponent + (bit_value - 0.5) * tilts[qubit_no]
    magnitude = jnp.exp(ramp * (0.55 + 2.0 * exponent))
    return noise * magnitude[None, :]


def draw_damp_qubits(key, part):
    shuffled = jax.random.permutation(jax.random.fold_in(key, 29), LQ)
    return shuffled[:LAYERS * KRAUS].reshape(LAYERS, KRAUS).astype(jnp.int32)


def touch_ends(drawn, rng, least, high):
    longest = drawn.shape.index(max(drawn.shape))
    spots = []
    for shift in (0, 1):
        where = [jax.random.randint(jax.random.fold_in(rng, axis), (), 0, length) for axis, length in enumerate(drawn.shape)]
        where[longest] = (where[longest] + shift) % drawn.shape[longest]
        spots.append(tuple(where))
    return drawn.at[spots[0]].set(least).at[spots[1]].set(high)


def setup_inputs(seed: int = 0) -> dict:
    key_list = jax.random.split(jax.random.key(seed), 6)
    return {
        "initial_state": draw_initial_state(jax.random.fold_in(key_list[5], 71), 0),
        "gate_angles": jnp.clip(jax.random.uniform(key_list[1], (LAYERS, 3, QUBITS), jnp.float32, -3.140625, 3.140625), -3.140625, 3.140625),
        "damp_qubits": draw_damp_qubits(jax.random.fold_in(key_list[5], 71), 0),
        "kraus_branch": touch_ends((jax.random.randint(key_list[3], (LAYERS, KRAUS), 0, 5) < 2).astype(jnp.int32), jax.random.fold_in(key_list[3], 1), 0, 1),
        "damping": jnp.clip(jnp.exp(jax.random.uniform(key_list[4], (LAYERS, KRAUS), jnp.float32, math.log(0.1), math.log(0.6))), 0.1, 0.6),
    }


epsilon = 1e-06

def gate_table(angles):
    half_theta = angles[1] * 0.5
    cosine = jnp.cos(half_theta)
    sine = jnp.sin(half_theta)
    summed = (angles[0] + angles[2]) * 0.5
    differ = (angles[0] - angles[2]) * 0.5
    real_part = jnp.stack([jnp.stack([jnp.cos(summed) * cosine, -jnp.cos(differ) * sine]), jnp.stack([jnp.cos(differ) * sine, jnp.cos(summed) * cosine])])
    imag_part = jnp.stack([jnp.stack([-jnp.sin(summed) * cosine, jnp.sin(differ) * sine]), jnp.stack([jnp.sin(differ) * sine, jnp.sin(summed) * cosine])])
    return (real_part, imag_part)

def complex_times(coef_re, coef_im, values):
    return jnp.stack([coef_re * values[0] - coef_im * values[1], coef_re * values[1] + coef_im * values[0]])

def apply_gate(amplitudes, position, real_part, imag_part):
    total = amplitudes.shape[1]
    viewed = amplitudes.reshape(2, total >> position + 1, 2, 1 << position)
    zero_half = viewed[:, :, 0]
    one_half = viewed[:, :, 1]
    new_zero = complex_times(real_part[0, 0], imag_part[0, 0], zero_half) + complex_times(real_part[0, 1], imag_part[0, 1], one_half)
    new_one = complex_times(real_part[1, 0], imag_part[1, 0], zero_half) + complex_times(real_part[1, 1], imag_part[1, 1], one_half)
    return jnp.stack([new_zero, new_one], axis=2).reshape(2, total)

def damp_step(amplitudes, target, rate, branch):
    total = amplitudes.shape[1]
    positions = lax.iota(jnp.int32, total)
    low_bit = jnp.bitwise_and(jnp.right_shift(positions, target), 1) == 0
    stride = jnp.left_shift(jnp.int32(1), target)
    shifted = jnp.roll(amplitudes, -stride, axis=1)
    lowered = jnp.where(low_bit, jnp.sqrt(rate) * shifted, jnp.zeros_like(amplitudes))
    kept = jnp.where(low_bit, amplitudes, jnp.sqrt(1.0 - rate) * amplitudes)
    return jnp.where(branch == 1, lowered, kept)

def reference(initial_state, gate_angles, damp_qubits, kraus_branch, damping):
    amplitudes = initial_state
    weights = []
    for layer_no in range(LAYERS):
        real_part, imag_part = gate_table(gate_angles[layer_no])
        for qubit_no in range(QUBITS):
            amplitudes = apply_gate(amplitudes, qubit_no, real_part[:, :, qubit_no], imag_part[:, :, qubit_no])
        for slot_no in range(KRAUS):
            before = jnp.sum(amplitudes * amplitudes) / AMPS
            damped = damp_step(amplitudes, damp_qubits[layer_no, slot_no], damping[layer_no, slot_no], kraus_branch[layer_no, slot_no])
            after = jnp.sum(damped * damped) / AMPS
            weights.append(after / before)
            amplitudes = damped * lax.rsqrt(after + epsilon)
    return (amplitudes, jnp.stack(weights).reshape(LAYERS, KRAUS))
```

```python
import functools
import heapq

import jax
import jax.numpy as jnp
from jax import lax
from jax.experimental import pallas as pl
from jax.experimental.pallas import tpu as pltpu
from jax.sharding import PartitionSpec as P

epsilon = 1e-06
LANE_BITS = 7
MESH = pl.DeviceIdType.MESH


def gate_entries(angles):
    half_theta = angles[1] * 0.5
    cosine = jnp.cos(half_theta)
    sine = jnp.sin(half_theta)
    summed = (angles[0] + angles[2]) * 0.5
    differ = (angles[0] - angles[2]) * 0.5
    cos_sum, sin_sum = jnp.cos(summed), jnp.sin(summed)
    cos_dif, sin_dif = jnp.cos(differ), jnp.sin(differ)
    real = [cos_sum * cosine, -cos_dif * sine, cos_dif * sine, cos_sum * cosine]
    imag = [-sin_sum * cosine, sin_dif * sine, sin_dif * sine, sin_sum * cosine]
    return (real, imag)


def product(left, right):
    lr, li = left
    rr, ri = right
    real, imag = [], []
    for row in range(2):
        for col in range(2):
            real.append(
                lr[2 * row] * rr[col]
                - li[2 * row] * ri[col]
                + lr[2 * row + 1] * rr[2 + col]
                - li[2 * row + 1] * ri[2 + col]
            )
            imag.append(
                lr[2 * row] * ri[col]
                + li[2 * row] * rr[col]
                + lr[2 * row + 1] * ri[2 + col]
                + li[2 * row + 1] * rr[2 + col]
            )
    return (real, imag)


def real_times(left, right):
    rr, ri = right
    real, imag = [], []
    for row in range(2):
        for col in range(2):
            real.append(left[2 * row] * rr[col] + left[2 * row + 1] * rr[2 + col])
            imag.append(left[2 * row] * ri[col] + left[2 * row + 1] * ri[2 + col])
    return (real, imag)


def kraus_entries(qubits, targets, branches, rates):
    ids = lax.iota(jnp.int32, qubits)
    one = jnp.ones((qubits,), jnp.float32)
    zero = jnp.zeros((qubits,), jnp.float32)
    entries = [one, zero, zero, one]
    for slot in range(targets.shape[0]):
        here = ids == targets[slot]
        jump = branches[slot] == 1
        keep = jnp.sqrt(1.0 - rates[slot])
        drop = jnp.sqrt(rates[slot])
        values = [
            jnp.where(jump, 0.0, 1.0),
            jnp.where(jump, drop, 0.0),
            0.0,
            jnp.where(jump, 0.0, keep),
        ]
        entries = [jnp.where(here, v, e) for v, e in zip(values, entries)]
    return entries


def tables(gate_angles, damp_qubits, kraus_branch, damping):
    layers, _, qubits = gate_angles.shape
    rows = []
    total = None
    for layer in range(layers):
        gates = gate_entries(gate_angles[layer])
        total = gates if total is None else product(gates, total)
        kraus = kraus_entries(qubits, damp_qubits[layer], kraus_branch[layer], damping[layer])
        total = real_times(kraus, total)
        rows += total[0] + total[1]
    return jnp.stack(rows)


def plan(bits, heavy, pieces):
    rest = [b for b in bits if b not in heavy]
    orders = []
    for p in range(pieces):
        flip = p % 2
        if len(heavy) == 2:
            order = [heavy[flip]] + (rest[::-1] if flip else rest) + [heavy[1 - flip]]
        else:
            order = bits[p % len(bits):] + bits[:p % len(bits)]
        orders.append(order)
    free = {b: 0.0 for b in bits}
    events = []
    queue = []

    def launch(p, step, now):
        b = orders[p][step]
        cost = 2.8 if b in heavy else (0.3 if b == 0 else 1.4)
        free[b] = max(free[b], now) + cost
        heapq.heappush(queue, (free[b] + 1.5, p, step))

    for p in range(pieces):
        launch(p, 0, 0.2 * (p // 4))
    while queue:
        now, p, step = heapq.heappop(queue)
        events.append((p, step))
        if step + 1 < len(bits):
            launch(p, step + 1, now)
    return orders, events


def split(values):
    high = values.astype(jnp.bfloat16)
    low = (values - high.astype(jnp.float32)).astype(jnp.bfloat16)
    return high, low


def matmul3(a_high, a_low, b_high, b_low):
    dot = functools.partial(jnp.dot, preferred_element_type=jnp.float32)
    return dot(a_high, b_high) + (dot(a_high, b_low) + dot(a_low, b_high))


def kernel(cfg, tab, damp, x_hbm, out_hbm, info_ref, x_ref, out_ref, planes, topped, stage, recv, mats,
           stats, stat_recv, send_sem, recv_sem, stat_send, stat_got, in_sem, out_sem):
    lo_bits, bits = cfg["lo_bits"], cfg["bits"]
    tiles, pieces, piece_rows = cfg["tiles"], cfg["pieces"], cfg["piece_rows"]
    local_bits, layers, slots = cfg["local_bits"], cfg["layers"], cfg["slots"]
    chunks = tiles // 16
    top_bits = chunks.bit_length() - 1
    orders, events = cfg["orders"], cfg["events"]
    last = 8 * (layers - 1)
    me = {"hi": lax.axis_index("hi"), "lo": lax.axis_index("lo")}

    def partner(b):
        axis, apart = ("lo", 1 << b) if b < lo_bits else ("hi", 1 << (b - lo_bits))
        bit = (me[axis] // apart) % 2
        return bit, {axis: me[axis] + apart * (1 - 2 * bit)}

    where_to = {b: partner(b) for b in bits}

    load = pltpu.make_async_copy(x_hbm, x_ref.at[pl.ds(0, 16 * tiles)], in_sem)
    load.start()
    barrier = pltpu.get_barrier_semaphore()
    for b in bits:
        pl.semaphore_signal(barrier, inc=1, device_id=where_to[b][1], device_id_type=MESH)

    def gate(q):
        return [tab[last + e, q] for e in range(8)]

    def build(first, transposed):
        shape = (128, 128)
        row = lax.broadcasted_iota(jnp.int32, shape, 1 if transposed else 0)
        col = lax.broadcasted_iota(jnp.int32, shape, 0 if transposed else 1)
        re = im = None
        for n in range(LANE_BITS):
            g = gate(first + n)
            rb = (row & (1 << n)) != 0
            cb = (col & (1 << n)) != 0
            er = jnp.where(rb, jnp.where(cb, g[3], g[2]), jnp.where(cb, g[1], g[0]))
            ei = jnp.where(rb, jnp.where(cb, g[7], g[6]), jnp.where(cb, g[5], g[4]))
            if re is None:
                re, im = er, ei
            else:
                re, im = re * er - im * ei, re * ei + im * er
        return re, im

    for slot, transposed in ((0, False), (1, True)):
        re, im = build(LANE_BITS * (1 - slot), transposed)
        sign = -1.0 if transposed else 1.0
        quads = ((re, -sign * im), (sign * im, re))
        for r in range(2):
            for c in range(2):
                high, low = split(quads[r][c])
                at = (pl.ds(128 * r, 128), pl.ds(128 * c, 128))
                mats[(2 * slot,) + at] = high
                mats[(2 * slot + 1,) + at] = low

    top_gates = [gate(2 * LANE_BITS + n) for n in range(top_bits)]

    def top_body(i, acc):
        vals = []
        for c in range(chunks):
            base = pl.multiple_of((c * 16 + i) * 16, 16)
            re = x_ref[pl.ds(base, 8, stride=2), :]
            im = x_ref[pl.ds(base + 1, 8, stride=2), :]
            planes[0, 0, c * 16 + i] = re
            planes[0, 1, c * 16 + i] = im
            acc = acc + (re * re + im * im)
            vals.append((re, im))
        for n in range(top_bits):
            g = top_gates[n]
            new = list(vals)
            for c in range(chunks):
                if c >> n & 1:
                    continue
                d = c | 1 << n
                (ar, ai), (br, bi) = vals[c], vals[d]
                new[c] = (
                    g[0] * ar - g[4] * ai + (g[1] * br - g[5] * bi),
                    g[0] * ai + g[4] * ar + (g[1] * bi + g[5] * br),
                )
                new[d] = (
                    g[2] * ar - g[6] * ai + (g[3] * br - g[7] * bi),
                    g[2] * ai + g[6] * ar + (g[3] * bi + g[7] * br),
                )
            vals = new
        at = pl.ds(pl.multiple_of(i * 8, 8), 8)
        for c in range(chunks):
            topped[c, 0, at, :] = vals[c][0]
            topped[c, 1, at, :] = vals[c][1]
        return acc

    load.wait()
    acc = lax.fori_loop(0, 16, top_body, jnp.zeros((8, 128), jnp.float32))
    stats[0] = jnp.zeros_like(stats[0])
    stats[0, 0:1, :] = jnp.sum(acc, axis=0, keepdims=True)

    pl.semaphore_wait(barrier, len(bits))

    copies = {}
    stores = []

    def launch(p, step):
        b = orders[p][step]
        copy = pltpu.make_async_remote_copy(
            src_ref=stage.at[step, p],
            dst_ref=recv.at[step, p],
            send_sem=send_sem.at[step, p],
            recv_sem=recv_sem.at[step, p],
            device_id=where_to[b][1],
            device_id_type=MESH,
        )
        copy.start()
        copies[p, step] = copy

    per_chunk = 128 // piece_rows
    for pair in range(chunks // 2):
        c, d = 2 * pair, 2 * pair + 1
        x = jnp.concatenate(
            [
                jnp.concatenate([topped[c, 0], topped[d, 0]], axis=1),
                jnp.concatenate([topped[c, 1], topped[d, 1]], axis=1),
            ],
            axis=0,
        )
        y = matmul3(mats[0], mats[1], *split(x))
        y = jnp.concatenate(
            [
                jnp.concatenate([y[:128, :128], y[128:, :128]], axis=1),
                jnp.concatenate([y[:128, 128:], y[128:, 128:]], axis=1),
            ],
            axis=0,
        )
        z = matmul3(*split(y), mats[2], mats[3])
        for k in range(2 * per_chunk):
            p = 2 * per_chunk * pair + k
            rows = slice(piece_rows * k, piece_rows * (k + 1))
            stage[0, p, 0] = z[rows, :128]
            stage[0, p, 1] = z[rows, 128:]
            launch(p, 0)

    coefs = {}
    for b in bits:
        g = gate(local_bits + b)
        one = where_to[b][0] == 1
        coefs[b] = (
            jnp.where(one, g[3], g[0]),
            jnp.where(one, g[7], g[4]),
            jnp.where(one, g[2], g[1]),
            jnp.where(one, g[6], g[5]),
        )

    def finish(p, step):
        copies[p, step].wait()
        cr, ci, dr, di = coefs[orders[p][step]]
        xr, xi = stage[step, p, 0], stage[step, p, 1]
        yr, yi = recv[step, p, 0], recv[step, p, 1]
        zr = (cr * xr - ci * xi) + (dr * yr - di * yi)
        zi = (cr * xi + ci * xr) + (dr * yi + di * yr)
        if step + 1 < len(bits):
            stage[step + 1, p, 0] = zr
            stage[step + 1, p, 1] = zi
            launch(p, step + 1)
        else:
            base = 2 * piece_rows * p
            out_ref[pl.ds(base, piece_rows, stride=2), :] = zr
            out_ref[pl.ds(base + 1, piece_rows, stride=2), :] = zi
            at = pl.ds(base, 2 * piece_rows)
            store = pltpu.make_async_copy(out_ref.at[at], out_hbm.at[at], out_sem.at[p])
            store.start()
            stores.append(store)

    lane = lax.broadcasted_iota(jnp.int32, (8, 128), 1)
    within = lax.broadcasted_iota(jnp.int32, (8, 128), 0) * 128 + lane

    def stat_step(j):
        src, dst = j % 2, (j + 1) % 2
        layer = j // slots
        t = damp[layer, j % slots]
        g = [tab[8 * layer + e, t] for e in range(8)]
        mask, lane_move, sub_move, tile_move = [damp[layers * (1 + m) + layer, j % slots] for m in range(4)]
        lane_up, sub_up = (128 - lane_move) & 127, (8 - sub_move) & 7
        lane_low = (within & lane_move) == 0
        sub_low = (within & (sub_move << 7)) == 0

        def meet(v):
            v = jnp.where(lane_low, pltpu.roll(v, lane_up, 1), pltpu.roll(v, lane_move, 1))
            return jnp.where(sub_low, pltpu.roll(v, sub_up, 0), pltpu.roll(v, sub_move, 0))

        def body(k, acc):
            for u in range(8):
                i = k * 8 + u
                other = i + tile_move - 2 * (i & tile_move)
                xr, xi = planes[src, 0, i], planes[src, 1, i]
                yr, yi = meet(planes[src, 0, other]), meet(planes[src, 1, other])
                bit = ((within + i * 1024) & mask) != 0
                cr, ci = jnp.where(bit, g[3], g[0]), jnp.where(bit, g[7], g[4])
                dr, di = jnp.where(bit, g[2], g[1]), jnp.where(bit, g[6], g[5])
                zr = (cr * xr - ci * xi) + (dr * yr - di * yi)
                zi = (cr * xi + ci * xr) + (dr * yi + di * yr)
                planes[dst, 0, i] = zr
                planes[dst, 1, i] = zi
                acc = acc + (zr * zr + zi * zi)
            return acc

        acc = lax.fori_loop(0, tiles // 8, body, jnp.zeros((8, 128), jnp.float32))
        stats[0, j + 1:j + 2, :] = jnp.sum(acc, axis=0, keepdims=True)

    stat_copies = {}

    def stat_launch(k):
        copy = pltpu.make_async_remote_copy(
            src_ref=stats.at[k],
            dst_ref=stat_recv.at[k],
            send_sem=stat_send.at[k],
            recv_sem=stat_got.at[k],
            device_id=where_to[bits[k]][1],
            device_id_type=MESH,
        )
        copy.start()
        stat_copies[k] = copy

    def stat_finish(k):
        stat_copies[k].wait()
        stats[k + 1] = stats[k] + stat_recv[k]

    def totals():
        summed = jnp.sum(stats[len(bits)], axis=1, keepdims=True) * (1.0 / cfg["whole"])
        factor = jnp.ones((1, 1), jnp.float32)
        info_ref[...] = jnp.zeros_like(info_ref)
        for j in range(layers * slots):
            before = summed[j:j + 1] * factor * factor
            after = summed[j + 1:j + 2] * factor * factor
            info_ref[j:j + 1, :] = jnp.broadcast_to(after / before, (1, 128))
            factor = factor * lax.rsqrt(after + epsilon)
        info_ref[layers * slots:layers * slots + 1, :] = jnp.broadcast_to(factor, (1, 128))

    jobs = [functools.partial(stat_step, j) for j in range(layers * slots)]
    gap = max(1, len(events) // (len(bits) + 2))
    done = 0
    for n, (p, step) in enumerate(events):
        if n < len(jobs):
            jobs[n]()
        finish(p, step)
        if n + 1 >= max(gap * (done + 1), len(jobs)) and done <= len(bits):
            if done > 0:
                stat_finish(done - 1)
            if done < len(bits):
                stat_launch(done)
            else:
                totals()
            done += 1
    assert done == len(bits) + 1
    for store in stores:
        store.wait()


def on_device(initial_state, gate_angles, damp_qubits, kraus_branch, damping):
    local_amps = initial_state.shape[1]
    local_bits = local_amps.bit_length() - 1
    hi, lo = lax.axis_size("hi"), lax.axis_size("lo")
    lo_bits, hi_bits = lo.bit_length() - 1, hi.bit_length() - 1
    bits = list(range(lo_bits + hi_bits))
    rows = local_amps >> LANE_BITS
    pieces = 16
    piece_rows = rows // pieces
    orders, events = plan(bits, [b for b in (1, 2) if b in bits], pieces)
    layers, slots = damp_qubits.shape
    cfg = dict(
        lo_bits=lo_bits, bits=bits, tiles=rows // 8, pieces=pieces, piece_rows=piece_rows,
        local_bits=local_bits, layers=layers, slots=slots, orders=orders, events=events,
        whole=float(local_amps * hi * lo),
    )
    mask = jnp.left_shift(jnp.int32(1), damp_qubits)
    moves = jnp.concatenate([damp_qubits, mask, mask & 127, (mask >> 7) & 7, mask >> 10])
    tab = tables(gate_angles, damp_qubits, kraus_branch, damping)
    x = initial_state.reshape(2, rows, 128).transpose(1, 0, 2).reshape(2 * rows, 128)
    count = len(bits)
    stat_rows = -(-(layers * slots + 1) // 8) * 8
    vmem = pl.BlockSpec(memory_space=pltpu.VMEM)
    whole = pl.BlockSpec(memory_space=pl.ANY)
    smem = pl.BlockSpec(memory_space=pltpu.SMEM)
    out, info = pl.pallas_call(
        functools.partial(kernel, cfg),
        out_shape=(
            jax.ShapeDtypeStruct((2 * rows, 128), jnp.float32),
            jax.ShapeDtypeStruct((stat_rows, 128), jnp.float32),
        ),
        in_specs=[smem, smem, whole],
        out_specs=(whole, vmem),
        scratch_shapes=[
            pltpu.VMEM((2 * rows + 8, 128), jnp.float32),
            pltpu.VMEM((2 * rows + 8, 128), jnp.float32),
            pltpu.VMEM((2, 2, rows // 8, 8, 128), jnp.float32),
            pltpu.VMEM((rows // 128, 2, 128, 128), jnp.float32),
            pltpu.VMEM((count, pieces, 2, piece_rows, 128), jnp.float32),
            pltpu.VMEM((count, pieces, 2, piece_rows, 128), jnp.float32),
            pltpu.VMEM((4, 256, 256), jnp.bfloat16),
            pltpu.VMEM((count + 1, stat_rows, 128), jnp.float32),
            pltpu.VMEM((count, stat_rows, 128), jnp.float32),
            pltpu.SemaphoreType.DMA((count, pieces)),
            pltpu.SemaphoreType.DMA((count, pieces)),
            pltpu.SemaphoreType.DMA((count,)),
            pltpu.SemaphoreType.DMA((count,)),
            pltpu.SemaphoreType.DMA,
            pltpu.SemaphoreType.DMA((pieces,)),
        ],
        compiler_params=pltpu.CompilerParams(
            collective_id=0, has_side_effects=True, vmem_limit_bytes=56 * 1024 * 1024
        ),
    )(tab, moves, x)
    amplitudes = out * info[layers * slots, 0]
    amplitudes = amplitudes.reshape(rows, 2, 128).transpose(1, 0, 2).reshape(2, local_amps)
    weights = info[:layers * slots, 0].reshape(layers, slots)
    return (amplitudes, weights)


def solution(mesh):
    in_specs = (P(None, ("hi", "lo")), P(), P(), P(), P())
    out_specs = (P(None, ("hi", "lo")), P())
    return jax.shard_map(
        on_device, mesh=mesh, in_specs=in_specs, out_specs=out_specs, check_vma=False
    )
```

```python
import functools
import heapq

import jax
import jax.numpy as jnp
from jax import lax
from jax.experimental import pallas as pl
from jax.experimental.pallas import tpu as pltpu
from jax.sharding import PartitionSpec as P

epsilon = 1e-06
LANE_BITS = 7
MESH = pl.DeviceIdType.MESH


def sine_cosine(angle):
    half = angle * 0.5
    square = half * half
    sine = 1.0 / 6227020800.0
    cosine = -1.0 / 87178291200.0
    for term in (-1.0 / 39916800.0, 1.0 / 362880.0, -1.0 / 5040.0, 1.0 / 120.0, -1.0 / 6.0, 1.0):
        sine = sine * square + term
    for term in (1.0 / 479001600.0, -1.0 / 3628800.0, 1.0 / 40320.0, -1.0 / 720.0, 1.0 / 24.0, -0.5, 1.0):
        cosine = cosine * square + term
    sine = sine * half
    return (2.0 * sine * cosine, 1.0 - 2.0 * sine * sine)


def gate_entries(a, b, c):
    sine, cosine = sine_cosine(b * 0.5)
    sin_sum, cos_sum = sine_cosine((a + c) * 0.5)
    sin_dif, cos_dif = sine_cosine((a - c) * 0.5)
    real = [cos_sum * cosine, -cos_dif * sine, cos_dif * sine, cos_sum * cosine]
    imag = [-sin_sum * cosine, sin_dif * sine, sin_dif * sine, sin_sum * cosine]
    return (real, imag)


def product(left, right):
    lr, li = left
    rr, ri = right
    real, imag = [], []
    for row in range(2):
        for col in range(2):
            real.append(
                lr[2 * row] * rr[col]
                - li[2 * row] * ri[col]
                + lr[2 * row + 1] * rr[2 + col]
                - li[2 * row + 1] * ri[2 + col]
            )
            imag.append(
                lr[2 * row] * ri[col]
                + li[2 * row] * rr[col]
                + lr[2 * row + 1] * ri[2 + col]
                + li[2 * row + 1] * rr[2 + col]
            )
    return (real, imag)


def real_times(left, right):
    rr, ri = right
    real, imag = [], []
    for row in range(2):
        for col in range(2):
            real.append(left[2 * row] * rr[col] + left[2 * row + 1] * rr[2 + col])
            imag.append(left[2 * row] * ri[col] + left[2 * row + 1] * ri[2 + col])
    return (real, imag)


def kraus_entries(shape, targets, branches, rates):
    ids = lax.broadcasted_iota(jnp.int32, shape, 1)
    one = jnp.ones(shape, jnp.float32)
    zero = jnp.zeros(shape, jnp.float32)
    entries = [one, zero, zero, one]
    for target, branch, rate in zip(targets, branches, rates):
        here = ids == target
        jump = jnp.full(shape, branch, jnp.int32) == 1
        rate = jnp.full(shape, rate, jnp.float32)
        values = [
            jnp.where(jump, zero, one),
            jnp.where(jump, jnp.sqrt(rate), zero),
            zero,
            jnp.where(jump, zero, jnp.sqrt(1.0 - rate)),
        ]
        entries = [jnp.where(here, v, e) for v, e in zip(values, entries)]
    return entries


def tables(angles, targets, branches, rates):
    layers, _, qubits = angles.shape
    slots = targets.shape[1]
    rows = []
    total = None
    for layer in range(layers):
        gates = gate_entries(*[angles[layer, k:k + 1, :] for k in range(3)])
        total = gates if total is None else product(gates, total)
        picked = [[ref[layer, slot] for slot in range(slots)] for ref in (targets, branches, rates)]
        kraus = kraus_entries((1, qubits), *picked)
        total = real_times(kraus, total)
        rows += total[0] + total[1]
    return rows


def plan(bits, heavy, pieces):
    rest = [b for b in bits if b not in heavy]
    orders = []
    for p in range(pieces):
        flip = p % 2
        if len(heavy) == 2:
            order = [heavy[flip]] + (rest[::-1] if flip else rest) + [heavy[1 - flip]]
        else:
            order = bits[p % len(bits):] + bits[:p % len(bits)]
        orders.append(order)
    free = {b: 0.0 for b in bits}
    events = []
    queue = []

    def launch(p, step, now):
        b = orders[p][step]
        cost = 2.8 if b in heavy else (0.3 if b == 0 else 1.4)
        free[b] = max(free[b], now) + cost
        heapq.heappush(queue, (free[b] + 1.5, p, step))

    for p in range(pieces):
        launch(p, 0, 0.2 * (p // 4))
    while queue:
        now, p, step = heapq.heappop(queue)
        events.append((p, step))
        if step + 1 < len(bits):
            launch(p, step + 1, now)
    return orders, events


def split(values):
    high = values.astype(jnp.bfloat16)
    low = (values - high.astype(jnp.float32)).astype(jnp.bfloat16)
    return high, low


def matmul3(a_high, a_low, b_high, b_low):
    dot = functools.partial(jnp.dot, preferred_element_type=jnp.float32)
    return dot(a_high, b_high) + (dot(a_high, b_low) + dot(a_low, b_high))


def kernel(cfg, angles, damp, branches, rates, x_hbm, out_hbm, info_ref, x_ref, out_ref, planes_a, planes_b, topped, stage, recv, mats,
           stats, stat_recv, send_sem, recv_sem, stat_send, stat_got, in_sem, out_sem,
           tab_rows, tab, tab_sem):
    lo_bits, bits = cfg["lo_bits"], cfg["bits"]
    tiles, pieces, piece_rows = cfg["tiles"], cfg["pieces"], cfg["piece_rows"]
    local_bits, layers, slots = cfg["local_bits"], cfg["layers"], cfg["slots"]
    chunks = tiles // 16
    top_bits = chunks.bit_length() - 1
    orders, events = cfg["orders"], cfg["events"]
    last = 8 * (layers - 1)
    me = {"hi": lax.axis_index("hi"), "lo": lax.axis_index("lo")}

    def partner(b):
        axis, apart = ("lo", 1 << b) if b < lo_bits else ("hi", 1 << (b - lo_bits))
        bit = (me[axis] // apart) % 2
        return bit, {axis: me[axis] + apart * (1 - 2 * bit)}

    where_to = {b: partner(b) for b in bits}

    load = pltpu.make_async_copy(x_hbm, x_ref.at[pl.ds(0, 16 * tiles)], in_sem)
    load.start()
    barrier = pltpu.get_barrier_semaphore()
    for b in bits:
        pl.semaphore_signal(barrier, inc=1, device_id=where_to[b][1], device_id_type=MESH)

    tab_rows[...] = jnp.zeros_like(tab_rows)
    for n, row in enumerate(tables(angles, damp, branches, rates)):
        tab_rows[n:n + 1, :angles.shape[2]] = row
    share = pltpu.make_async_copy(tab_rows, tab, tab_sem)
    share.start()
    share.wait()

    def gate(q):
        return [tab[last + e, q] for e in range(8)]

    def build(first, transposed):
        shape = (128, 128)
        row = lax.broadcasted_iota(jnp.int32, shape, 1 if transposed else 0)
        col = lax.broadcasted_iota(jnp.int32, shape, 0 if transposed else 1)
        re = im = None
        for n in range(LANE_BITS):
            g = gate(first + n)
            rb = (row & (1 << n)) != 0
            cb = (col & (1 << n)) != 0
            er = jnp.where(rb, jnp.where(cb, g[3], g[2]), jnp.where(cb, g[1], g[0]))
            ei = jnp.where(rb, jnp.where(cb, g[7], g[6]), jnp.where(cb, g[5], g[4]))
            if re is None:
                re, im = er, ei
            else:
                re, im = re * er - im * ei, re * ei + im * er
        return re, im

    for slot, transposed in ((0, False), (1, True)):
        re, im = build(LANE_BITS * (1 - slot), transposed)
        sign = -1.0 if transposed else 1.0
        quads = ((re, -sign * im), (sign * im, re))
        for r in range(2):
            for c in range(2):
                high, low = split(quads[r][c])
                at = (pl.ds(128 * r, 128), pl.ds(128 * c, 128))
                mats[(2 * slot,) + at] = high
                mats[(2 * slot + 1,) + at] = low

    top_gates = [gate(2 * LANE_BITS + n) for n in range(top_bits)]

    def top_body(i, acc):
        vals = []
        for c in range(chunks):
            base = pl.multiple_of((c * 16 + i) * 16, 16)
            re = x_ref[pl.ds(base, 8, stride=2), :]
            im = x_ref[pl.ds(base + 1, 8, stride=2), :]
            planes_a[0, c * 16 + i] = re
            planes_a[1, c * 16 + i] = im
            acc = acc + (re * re + im * im)
            vals.append((re, im))
        for n in range(top_bits):
            g = top_gates[n]
            new = list(vals)
            for c in range(chunks):
                if c >> n & 1:
                    continue
                d = c | 1 << n
                (ar, ai), (br, bi) = vals[c], vals[d]
                new[c] = (
                    g[0] * ar - g[4] * ai + (g[1] * br - g[5] * bi),
                    g[0] * ai + g[4] * ar + (g[1] * bi + g[5] * br),
                )
                new[d] = (
                    g[2] * ar - g[6] * ai + (g[3] * br - g[7] * bi),
                    g[2] * ai + g[6] * ar + (g[3] * bi + g[7] * br),
                )
            vals = new
        at = pl.ds(pl.multiple_of(i * 8, 8), 8)
        for c in range(chunks):
            topped[c, 0, at, :] = vals[c][0]
            topped[c, 1, at, :] = vals[c][1]
        return acc

    load.wait()
    acc = lax.fori_loop(0, 16, top_body, jnp.zeros((8, 128), jnp.float32))
    stats[0] = jnp.zeros_like(stats[0])
    stats[0, 0:1, :] = jnp.sum(acc, axis=0, keepdims=True)

    pl.semaphore_wait(barrier, len(bits))

    copies = {}
    stores = []

    def launch(p, step):
        b = orders[p][step]
        copy = pltpu.make_async_remote_copy(
            src_ref=stage.at[step, p],
            dst_ref=recv.at[step, p],
            send_sem=send_sem.at[step, p],
            recv_sem=recv_sem.at[step, p],
            device_id=where_to[b][1],
            device_id_type=MESH,
        )
        copy.start()
        copies[p, step] = copy

    per_chunk = 128 // piece_rows
    for pair in range(chunks // 2):
        c, d = 2 * pair, 2 * pair + 1
        x = jnp.concatenate(
            [
                jnp.concatenate([topped[c, 0], topped[d, 0]], axis=1),
                jnp.concatenate([topped[c, 1], topped[d, 1]], axis=1),
            ],
            axis=0,
        )
        y = matmul3(mats[0], mats[1], *split(x))
        y = jnp.concatenate(
            [
                jnp.concatenate([y[:128, :128], y[128:, :128]], axis=1),
                jnp.concatenate([y[:128, 128:], y[128:, 128:]], axis=1),
            ],
            axis=0,
        )
        z = matmul3(*split(y), mats[2], mats[3])
        for k in range(2 * per_chunk):
            p = 2 * per_chunk * pair + k
            rows = slice(piece_rows * k, piece_rows * (k + 1))
            stage[0, p, 0] = z[rows, :128]
            stage[0, p, 1] = z[rows, 128:]
            launch(p, 0)

    coefs = {}
    for b in bits:
        g = gate(local_bits + b)
        one = where_to[b][0] == 1
        coefs[b] = (
            jnp.where(one, g[3], g[0]),
            jnp.where(one, g[7], g[4]),
            jnp.where(one, g[2], g[1]),
            jnp.where(one, g[6], g[5]),
        )

    def finish(p, step):
        copies[p, step].wait()
        cr, ci, dr, di = coefs[orders[p][step]]
        xr, xi = stage[step, p, 0], stage[step, p, 1]
        yr, yi = recv[step, p, 0], recv[step, p, 1]
        zr = (cr * xr - ci * xi) + (dr * yr - di * yi)
        zi = (cr * xi + ci * xr) + (dr * yi + di * yr)
        if step + 1 < len(bits):
            stage[step + 1, p, 0] = zr
            stage[step + 1, p, 1] = zi
            launch(p, step + 1)
        else:
            base = 2 * piece_rows * p
            out_ref[pl.ds(base, piece_rows, stride=2), :] = zr
            out_ref[pl.ds(base + 1, piece_rows, stride=2), :] = zi
            at = pl.ds(base, 2 * piece_rows)
            store = pltpu.make_async_copy(out_ref.at[at], out_hbm.at[at], out_sem.at[p])
            store.start()
            stores.append(store)

    lane = lax.broadcasted_iota(jnp.int32, (8, 128), 1)
    within = lax.broadcasted_iota(jnp.int32, (8, 128), 0) * 128 + lane

    carry = {}
    parts, batch = cfg["parts"], cfg["batch"]

    def stat_step(j, part):
        src, dst = (planes_a, planes_b) if j % 2 == 0 else (planes_b, planes_a)
        layer = j // slots
        t = damp[layer, j % slots]
        g = [tab[8 * layer + e, t] for e in range(8)]

        def power(first, end, unit):
            value = jnp.int32(0)
            for n in range(first, end):
                value = jnp.where(t == n, jnp.int32(1 << (n - unit)), value)
            return value

        mask = power(0, local_bits, 0)
        lane_move, sub_move = power(0, 7, 0), power(7, 10, 7)
        tile_move = power(10, local_bits, 10)
        lane_up, sub_up = (128 - lane_move) & 127, (8 - sub_move) & 7
        lane_low = (within & lane_move) == 0
        sub_low = (within & (sub_move * 128)) == 0
        final = j + 1 == layers * slots

        def meet(v):
            v = jnp.where(lane_low, pltpu.roll(v, lane_up, 1), pltpu.roll(v, lane_move, 1))
            return jnp.where(sub_low, pltpu.roll(v, sub_up, 0), pltpu.roll(v, sub_move, 0))

        def body(k, acc):
            ids = [k * batch + u for u in range(batch)]
            others = [i + tile_move - 2 * (i & tile_move) for i in ids]
            xs = [(src[0, i], src[1, i]) for i in ids]
            ys = [(src[0, o], src[1, o]) for o in others]
            ys = [(meet(yr), meet(yi)) for yr, yi in ys]
            zs = []
            for i, (xr, xi), (yr, yi) in zip(ids, xs, ys):
                bit = ((within + i * 1024) & mask) != 0
                cr, ci = jnp.where(bit, g[3], g[0]), jnp.where(bit, g[7], g[4])
                dr, di = jnp.where(bit, g[2], g[1]), jnp.where(bit, g[6], g[5])
                zr = (cr * xr - ci * xi) + (dr * yr - di * yi)
                zi = (cr * xi + ci * xr) + (dr * yi + di * yr)
                zs.append((zr, zi))
            for i, (zr, zi) in zip(ids, zs):
                if not final:
                    dst[0, i] = zr
                    dst[1, i] = zi
            squares = [zr * zr + zi * zi for zr, zi in zs]
            while len(squares) > 1:
                squares = [u + v for u, v in zip(squares[::2], squares[1::2])]
            return acc + squares[0]

        steps = tiles // batch // parts
        acc = carry.pop(j, None)
        acc = jnp.zeros((8, 128), jnp.float32) if acc is None else acc
        acc = lax.fori_loop(part * steps, (part + 1) * steps, body, acc)
        if part + 1 < parts:
            carry[j] = acc
        else:
            stats[0, j + 1:j + 2, :] = jnp.sum(acc, axis=0, keepdims=True)

    stat_copies = {}

    def stat_launch(k):
        copy = pltpu.make_async_remote_copy(
            src_ref=stats.at[k],
            dst_ref=stat_recv.at[k],
            send_sem=stat_send.at[k],
            recv_sem=stat_got.at[k],
            device_id=where_to[bits[k]][1],
            device_id_type=MESH,
        )
        copy.start()
        stat_copies[k] = copy

    def stat_finish(k):
        stat_copies[k].wait()
        stats[k + 1] = stats[k] + stat_recv[k]

    def totals():
        summed = jnp.sum(stats[len(bits)], axis=1, keepdims=True) * (1.0 / cfg["whole"])
        factor = jnp.ones((1, 1), jnp.float32)
        info_ref[...] = jnp.zeros_like(info_ref)
        for j in range(layers * slots):
            before = summed[j:j + 1] * factor * factor
            after = summed[j + 1:j + 2] * factor * factor
            info_ref[j:j + 1, :] = jnp.broadcast_to(after / before, (1, 128))
            factor = factor * lax.rsqrt(after + epsilon)
        info_ref[layers * slots:layers * slots + 1, :] = jnp.broadcast_to(factor, (1, 128))

    jobs = [functools.partial(stat_step, j, part) for j in range(layers * slots) for part in range(parts)]
    per = -(-len(jobs) // max(1, len(events) // 3))
    ready = -(-len(jobs) // per)
    gap = max(1, (len(events) - ready) // (len(bits) + 1))
    done = 0
    for n, (p, step) in enumerate(events):
        for job in jobs[n * per:(n + 1) * per]:
            job()
        finish(p, step)
        if n + 1 >= ready + gap * done and done <= len(bits):
            if done > 0:
                stat_finish(done - 1)
            if done < len(bits):
                stat_launch(done)
            else:
                totals()
            done += 1
    assert done == len(bits) + 1
    for store in stores:
        store.wait()


def on_device(initial_state, gate_angles, damp_qubits, kraus_branch, damping):
    local_amps = initial_state.shape[1]
    local_bits = local_amps.bit_length() - 1
    hi, lo = lax.axis_size("hi"), lax.axis_size("lo")
    lo_bits, hi_bits = lo.bit_length() - 1, hi.bit_length() - 1
    bits = list(range(lo_bits + hi_bits))
    rows = local_amps >> LANE_BITS
    pieces = 16
    piece_rows = rows // pieces
    orders, events = plan(bits, [b for b in (1, 2) if b in bits], pieces)
    layers, slots = damp_qubits.shape
    cfg = dict(
        parts=2, batch=8,
        lo_bits=lo_bits, bits=bits, tiles=rows // 8, pieces=pieces, piece_rows=piece_rows,
        local_bits=local_bits, layers=layers, slots=slots, orders=orders, events=events,
        whole=float(local_amps * hi * lo),
    )
    x = initial_state.reshape(2, rows, 128).transpose(1, 0, 2).reshape(2 * rows, 128)
    count = len(bits)
    stat_rows = -(-(layers * slots + 1) // 8) * 8
    vmem = pl.BlockSpec(memory_space=pltpu.VMEM)
    whole = pl.BlockSpec(memory_space=pl.ANY)
    smem = pl.BlockSpec(memory_space=pltpu.SMEM)
    out, info = pl.pallas_call(
        functools.partial(kernel, cfg),
        out_shape=(
            jax.ShapeDtypeStruct((2 * rows, 128), jnp.float32),
            jax.ShapeDtypeStruct((stat_rows, 128), jnp.float32),
        ),
        in_specs=[vmem, smem, smem, smem, whole],
        out_specs=(whole, vmem),
        scratch_shapes=[
            pltpu.VMEM((2 * rows + 8, 128), jnp.float32),
            pltpu.VMEM((2 * rows + 8, 128), jnp.float32),
            pltpu.VMEM((2, rows // 8, 8, 128), jnp.float32),
            pltpu.VMEM((2, rows // 8, 8, 128), jnp.float32),
            pltpu.VMEM((rows // 128, 2, 128, 128), jnp.float32),
            pltpu.VMEM((count, pieces, 2, piece_rows, 128), jnp.float32),
            pltpu.VMEM((count, pieces, 2, piece_rows, 128), jnp.float32),
            pltpu.VMEM((4, 256, 256), jnp.bfloat16),
            pltpu.VMEM((count + 1, stat_rows, 128), jnp.float32),
            pltpu.VMEM((count, stat_rows, 128), jnp.float32),
            pltpu.SemaphoreType.DMA((count, pieces)),
            pltpu.SemaphoreType.DMA((count, pieces)),
            pltpu.SemaphoreType.DMA((count,)),
            pltpu.SemaphoreType.DMA((count,)),
            pltpu.SemaphoreType.DMA,
            pltpu.SemaphoreType.DMA((pieces,)),
            pltpu.VMEM((8 * layers, 128), jnp.float32),
            pltpu.SMEM((8 * layers, 128), jnp.float32),
            pltpu.SemaphoreType.DMA,
        ],
        compiler_params=pltpu.CompilerParams(
            collective_id=0, has_side_effects=True, vmem_limit_bytes=56 * 1024 * 1024
        ),
    )(gate_angles, damp_qubits, kraus_branch, damping, x)
    amplitudes = out * info[layers * slots, 0]
    amplitudes = amplitudes.reshape(rows, 2, 128).transpose(1, 0, 2).reshape(2, local_amps)
    weights = info[:layers * slots, 0].reshape(layers, slots)
    return (amplitudes, weights)


def solution(mesh):
    in_specs = (P(None, ("hi", "lo")), P(), P(), P(), P())
    out_specs = (P(None, ("hi", "lo")), P())
    return jax.shard_map(
        on_device, mesh=mesh, in_specs=in_specs, out_specs=out_specs, check_vma=False
    )
```

```python
import functools
import heapq

import jax
import jax.numpy as jnp
from jax import lax
from jax.experimental import pallas as pl
from jax.experimental.pallas import tpu as pltpu
from jax.sharding import PartitionSpec as P

epsilon = 1e-06
LANE_BITS = 7
MESH = pl.DeviceIdType.MESH


def sine_cosine(angle):
    half = angle * 0.5
    square = half * half
    sine = 1.0 / 6227020800.0
    cosine = -1.0 / 87178291200.0
    for term in (-1.0 / 39916800.0, 1.0 / 362880.0, -1.0 / 5040.0, 1.0 / 120.0, -1.0 / 6.0, 1.0):
        sine = sine * square + term
    for term in (1.0 / 479001600.0, -1.0 / 3628800.0, 1.0 / 40320.0, -1.0 / 720.0, 1.0 / 24.0, -0.5, 1.0):
        cosine = cosine * square + term
    sine = sine * half
    return (2.0 * sine * cosine, 1.0 - 2.0 * sine * sine)


def gate_entries(a, b, c):
    sine, cosine = sine_cosine(b * 0.5)
    sin_sum, cos_sum = sine_cosine((a + c) * 0.5)
    sin_dif, cos_dif = sine_cosine((a - c) * 0.5)
    real = [cos_sum * cosine, -cos_dif * sine, cos_dif * sine, cos_sum * cosine]
    imag = [-sin_sum * cosine, sin_dif * sine, sin_dif * sine, sin_sum * cosine]
    return (real, imag)


def product(left, right):
    lr, li = left
    rr, ri = right
    real, imag = [], []
    for row in range(2):
        for col in range(2):
            real.append(
                lr[2 * row] * rr[col]
                - li[2 * row] * ri[col]
                + lr[2 * row + 1] * rr[2 + col]
                - li[2 * row + 1] * ri[2 + col]
            )
            imag.append(
                lr[2 * row] * ri[col]
                + li[2 * row] * rr[col]
                + lr[2 * row + 1] * ri[2 + col]
                + li[2 * row + 1] * rr[2 + col]
            )
    return (real, imag)


def real_times(left, right):
    rr, ri = right
    real, imag = [], []
    for row in range(2):
        for col in range(2):
            real.append(left[2 * row] * rr[col] + left[2 * row + 1] * rr[2 + col])
            imag.append(left[2 * row] * ri[col] + left[2 * row + 1] * ri[2 + col])
    return (real, imag)


def kraus_entries(shape, targets, branches, rates):
    ids = lax.broadcasted_iota(jnp.int32, shape, 1)
    one = jnp.ones(shape, jnp.float32)
    zero = jnp.zeros(shape, jnp.float32)
    entries = [one, zero, zero, one]
    for target, branch, rate in zip(targets, branches, rates):
        here = ids == target
        jump = jnp.full(shape, branch, jnp.int32) == 1
        rate = jnp.full(shape, rate, jnp.float32)
        values = [
            jnp.where(jump, zero, one),
            jnp.where(jump, jnp.sqrt(rate), zero),
            zero,
            jnp.where(jump, zero, jnp.sqrt(1.0 - rate)),
        ]
        entries = [jnp.where(here, v, e) for v, e in zip(values, entries)]
    return entries


def tables(angles, targets, branches, rates):
    _, layers, qubits = angles.shape
    slots = targets.shape[1]
    rows = []
    total = None
    for layer in range(layers):
        gates = gate_entries(*[angles[k, layer:layer + 1, :] for k in range(3)])
        total = gates if total is None else product(gates, total)
        picked = [[ref[layer, slot] for slot in range(slots)] for ref in (targets, branches, rates)]
        kraus = kraus_entries((1, qubits), *picked)
        total = real_times(kraus, total)
        rows += total[0] + total[1]
    return rows


def plan(bits, heavy, pieces):
    rest = [b for b in bits if b not in heavy]
    orders = []
    for p in range(pieces):
        flip = p % 2
        if len(heavy) == 2:
            order = [heavy[flip]] + (rest[::-1] if flip else rest) + [heavy[1 - flip]]
        else:
            order = bits[p % len(bits):] + bits[:p % len(bits)]
        orders.append(order)
    free = {b: 0.0 for b in bits}
    events = []
    queue = []

    def launch(p, step, now):
        b = orders[p][step]
        cost = 2.8 if b in heavy else (0.3 if b == 0 else 1.4)
        free[b] = max(free[b], now) + cost
        heapq.heappush(queue, (free[b] + 1.5, p, step))

    for p in range(pieces):
        launch(p, 0, 0.2 * (p // 4))
    while queue:
        now, p, step = heapq.heappop(queue)
        events.append((p, step))
        if step + 1 < len(bits):
            launch(p, step + 1, now)
    return orders, events


def split(values):
    high = values.astype(jnp.bfloat16)
    low = (values - high.astype(jnp.float32)).astype(jnp.bfloat16)
    return high, low


def matmul3(a_high, a_low, b_high, b_low):
    dot = functools.partial(jnp.dot, preferred_element_type=jnp.float32)
    return dot(a_high, b_high) + (dot(a_high, b_low) + dot(a_low, b_high))


def kernel(cfg, angles, damp, branches, rates, x_hbm, out_hbm, info_ref, x_ref, out_ref, planes_a, planes_b, topped, stage, recv, mats,
           stats, stat_recv, send_sem, recv_sem, stat_send, stat_got, in_sem, out_sem,
           tab_rows, tab, tab_sem):
    lo_bits, bits = cfg["lo_bits"], cfg["bits"]
    tiles, pieces, piece_rows = cfg["tiles"], cfg["pieces"], cfg["piece_rows"]
    local_bits, layers, slots = cfg["local_bits"], cfg["layers"], cfg["slots"]
    chunks = tiles // 16
    top_bits = chunks.bit_length() - 1
    orders, events = cfg["orders"], cfg["events"]
    last = 8 * (layers - 1)
    me = {"hi": lax.axis_index("hi"), "lo": lax.axis_index("lo")}

    def partner(b):
        axis, apart = ("lo", 1 << b) if b < lo_bits else ("hi", 1 << (b - lo_bits))
        bit = (me[axis] // apart) % 2
        return bit, {axis: me[axis] + apart * (1 - 2 * bit)}

    where_to = {b: partner(b) for b in bits}

    load = pltpu.make_async_copy(x_hbm, x_ref.at[pl.ds(0, 16 * tiles)], in_sem)
    load.start()
    barrier = pltpu.get_barrier_semaphore()
    for b in bits:
        pl.semaphore_signal(barrier, inc=1, device_id=where_to[b][1], device_id_type=MESH)

    tab_rows[...] = jnp.zeros_like(tab_rows)
    for n, row in enumerate(tables(angles, damp, branches, rates)):
        tab_rows[n:n + 1, :angles.shape[2]] = row
    share = pltpu.make_async_copy(tab_rows, tab, tab_sem)
    share.start()
    share.wait()

    def gate(q):
        return [tab[last + e, q] for e in range(8)]

    def build(first, transposed):
        shape = (128, 128)
        row = lax.broadcasted_iota(jnp.int32, shape, 1 if transposed else 0)
        col = lax.broadcasted_iota(jnp.int32, shape, 0 if transposed else 1)
        re = im = None
        for n in range(LANE_BITS):
            g = gate(first + n)
            rb = (row & (1 << n)) != 0
            cb = (col & (1 << n)) != 0
            er = jnp.where(rb, jnp.where(cb, g[3], g[2]), jnp.where(cb, g[1], g[0]))
            ei = jnp.where(rb, jnp.where(cb, g[7], g[6]), jnp.where(cb, g[5], g[4]))
            if re is None:
                re, im = er, ei
            else:
                re, im = re * er - im * ei, re * ei + im * er
        return re, im

    for slot, transposed in ((0, False), (1, True)):
        re, im = build(LANE_BITS * (1 - slot), transposed)
        sign = -1.0 if transposed else 1.0
        quads = ((re, -sign * im), (sign * im, re))
        for r in range(2):
            for c in range(2):
                high, low = split(quads[r][c])
                at = (pl.ds(128 * r, 128), pl.ds(128 * c, 128))
                mats[(2 * slot,) + at] = high
                mats[(2 * slot + 1,) + at] = low

    top_gates = [gate(2 * LANE_BITS + n) for n in range(top_bits)]

    def top_body(i, acc):
        vals = []
        for c in range(chunks):
            base = pl.multiple_of((c * 16 + i) * 16, 16)
            re = x_ref[pl.ds(base, 8, stride=2), :]
            im = x_ref[pl.ds(base + 1, 8, stride=2), :]
            planes_a[0, c * 16 + i] = re
            planes_a[1, c * 16 + i] = im
            acc = acc + (re * re + im * im)
            vals.append((re, im))
        for n in range(top_bits):
            g = top_gates[n]
            new = list(vals)
            for c in range(chunks):
                if c >> n & 1:
                    continue
                d = c | 1 << n
                (ar, ai), (br, bi) = vals[c], vals[d]
                new[c] = (
                    g[0] * ar - g[4] * ai + (g[1] * br - g[5] * bi),
                    g[0] * ai + g[4] * ar + (g[1] * bi + g[5] * br),
                )
                new[d] = (
                    g[2] * ar - g[6] * ai + (g[3] * br - g[7] * bi),
                    g[2] * ai + g[6] * ar + (g[3] * bi + g[7] * br),
                )
            vals = new
        at = pl.ds(pl.multiple_of(i * 8, 8), 8)
        for c in range(chunks):
            topped[c, 0, at, :] = vals[c][0]
            topped[c, 1, at, :] = vals[c][1]
        return acc

    load.wait()
    acc = lax.fori_loop(0, 16, top_body, jnp.zeros((8, 128), jnp.float32))
    stats[0] = jnp.zeros_like(stats[0])
    stats[0, 0:1, :] = jnp.sum(acc, axis=0, keepdims=True)

    pl.semaphore_wait(barrier, len(bits))

    copies = {}
    stores = []

    def launch(p, step):
        b = orders[p][step]
        copy = pltpu.make_async_remote_copy(
            src_ref=stage.at[step, p],
            dst_ref=recv.at[step, p],
            send_sem=send_sem.at[step, p],
            recv_sem=recv_sem.at[step, p],
            device_id=where_to[b][1],
            device_id_type=MESH,
        )
        copy.start()
        copies[p, step] = copy

    per_chunk = 128 // piece_rows
    for pair in range(chunks // 2):
        c, d = 2 * pair, 2 * pair + 1
        x = jnp.concatenate(
            [
                jnp.concatenate([topped[c, 0], topped[d, 0]], axis=1),
                jnp.concatenate([topped[c, 1], topped[d, 1]], axis=1),
            ],
            axis=0,
        )
        y = matmul3(mats[0], mats[1], *split(x))
        y = jnp.concatenate(
            [
                jnp.concatenate([y[:128, :128], y[128:, :128]], axis=1),
                jnp.concatenate([y[:128, 128:], y[128:, 128:]], axis=1),
            ],
            axis=0,
        )
        z = matmul3(*split(y), mats[2], mats[3])
        for k in range(2 * per_chunk):
            p = 2 * per_chunk * pair + k
            rows = slice(piece_rows * k, piece_rows * (k + 1))
            stage[0, p, 0] = z[rows, :128]
            stage[0, p, 1] = z[rows, 128:]
            launch(p, 0)

    coefs = {}
    for b in bits:
        g = gate(local_bits + b)
        one = where_to[b][0] == 1
        coefs[b] = (
            jnp.where(one, g[3], g[0]),
            jnp.where(one, g[7], g[4]),
            jnp.where(one, g[2], g[1]),
            jnp.where(one, g[6], g[5]),
        )

    def finish(p, step):
        copies[p, step].wait()
        cr, ci, dr, di = coefs[orders[p][step]]
        xr, xi = stage[step, p, 0], stage[step, p, 1]
        yr, yi = recv[step, p, 0], recv[step, p, 1]
        zr = (cr * xr - ci * xi) + (dr * yr - di * yi)
        zi = (cr * xi + ci * xr) + (dr * yi + di * yr)
        if step + 1 < len(bits):
            stage[step + 1, p, 0] = zr
            stage[step + 1, p, 1] = zi
            launch(p, step + 1)
        else:
            base = 2 * piece_rows * p
            out_ref[pl.ds(base, piece_rows, stride=2), :] = zr
            out_ref[pl.ds(base + 1, piece_rows, stride=2), :] = zi
            at = pl.ds(base, 2 * piece_rows)
            store = pltpu.make_async_copy(out_ref.at[at], out_hbm.at[at], out_sem.at[p])
            store.start()
            stores.append(store)

    lane = lax.broadcasted_iota(jnp.int32, (8, 128), 1)
    within = lax.broadcasted_iota(jnp.int32, (8, 128), 0) * 128 + lane

    carry = {}
    parts, batch = cfg["parts"], cfg["batch"]

    def stat_step(j, part):
        src, dst = (planes_a, planes_b) if j % 2 == 0 else (planes_b, planes_a)
        layer = j // slots
        t = damp[layer, j % slots]
        g = [tab[8 * layer + e, t] for e in range(8)]

        def power(first, end, unit):
            value = jnp.int32(0)
            for n in range(first, end):
                value = jnp.where(t == n, jnp.int32(1 << (n - unit)), value)
            return value

        mask = power(0, local_bits, 0)
        lane_move, sub_move = power(0, 7, 0), power(7, 10, 7)
        tile_move = power(10, local_bits, 10)
        lane_up, sub_up = (128 - lane_move) & 127, (8 - sub_move) & 7
        lane_low = (within & lane_move) == 0
        sub_low = (within & (sub_move * 128)) == 0
        final = j + 1 == layers * slots

        def meet(v):
            v = jnp.where(lane_low, pltpu.roll(v, lane_up, 1), pltpu.roll(v, lane_move, 1))
            return jnp.where(sub_low, pltpu.roll(v, sub_up, 0), pltpu.roll(v, sub_move, 0))

        def body(k, acc):
            ids = [k * batch + u for u in range(batch)]
            others = [i + tile_move - 2 * (i & tile_move) for i in ids]
            xs = [(src[0, i], src[1, i]) for i in ids]
            ys = [(src[0, o], src[1, o]) for o in others]
            ys = [(meet(yr), meet(yi)) for yr, yi in ys]
            zs = []
            for i, (xr, xi), (yr, yi) in zip(ids, xs, ys):
                bit = ((within + i * 1024) & mask) != 0
                cr, ci = jnp.where(bit, g[3], g[0]), jnp.where(bit, g[7], g[4])
                dr, di = jnp.where(bit, g[2], g[1]), jnp.where(bit, g[6], g[5])
                zr = (cr * xr - ci * xi) + (dr * yr - di * yi)
                zi = (cr * xi + ci * xr) + (dr * yi + di * yr)
                zs.append((zr, zi))
            for i, (zr, zi) in zip(ids, zs):
                if not final:
                    dst[0, i] = zr
                    dst[1, i] = zi
            squares = [zr * zr + zi * zi for zr, zi in zs]
            while len(squares) > 1:
                squares = [u + v for u, v in zip(squares[::2], squares[1::2])]
            return acc + squares[0]

        steps = tiles // batch // parts
        acc = carry.pop(j, None)
        acc = jnp.zeros((8, 128), jnp.float32) if acc is None else acc
        acc = lax.fori_loop(part * steps, (part + 1) * steps, body, acc)
        if part + 1 < parts:
            carry[j] = acc
        else:
            stats[0, j + 1:j + 2, :] = jnp.sum(acc, axis=0, keepdims=True)

    stat_copies = {}

    def stat_launch(k):
        copy = pltpu.make_async_remote_copy(
            src_ref=stats.at[k],
            dst_ref=stat_recv.at[k],
            send_sem=stat_send.at[k],
            recv_sem=stat_got.at[k],
            device_id=where_to[bits[k]][1],
            device_id_type=MESH,
        )
        copy.start()
        stat_copies[k] = copy

    def stat_finish(k):
        stat_copies[k].wait()
        stats[k + 1] = stats[k] + stat_recv[k]

    def totals():
        summed = jnp.sum(stats[len(bits)], axis=1, keepdims=True) * (1.0 / cfg["whole"])
        factor = jnp.ones((1, 1), jnp.float32)
        info_ref[...] = jnp.zeros_like(info_ref)
        line = lax.broadcasted_iota(jnp.int32, (1, 128), 1)
        for layer in range(layers):
            weights = jnp.zeros((1, 128), jnp.float32)
            for slot in range(slots):
                j = layer * slots + slot
                before = summed[j:j + 1] * factor * factor
                after = summed[j + 1:j + 2] * factor * factor
                weights = jnp.where(line == slot, after / before, weights)
                factor = factor * lax.rsqrt(after + epsilon)
            info_ref[layer:layer + 1, :] = weights
        info_ref[layers:layers + 1, :] = jnp.broadcast_to(factor, (1, 128))

    jobs = [functools.partial(stat_step, j, part) for j in range(layers * slots) for part in range(parts)]
    per = -(-len(jobs) // max(1, len(events) // 3))
    ready = -(-len(jobs) // per)
    gap = max(1, (len(events) - ready) // (len(bits) + 1))
    done = 0
    for n, (p, step) in enumerate(events):
        for job in jobs[n * per:(n + 1) * per]:
            job()
        finish(p, step)
        if n + 1 >= ready + gap * done and done <= len(bits):
            if done > 0:
                stat_finish(done - 1)
            if done < len(bits):
                stat_launch(done)
            else:
                totals()
            done += 1
    assert done == len(bits) + 1
    for store in stores:
        store.wait()


def scale_kernel(blocks, info, x_hbm, out_hbm, weights, held, scaled, in_sem, out_sem):
    layers, slots = weights.shape
    size = held.shape[0] // blocks
    loads, stores = [], []
    for n in range(blocks):
        at = pl.ds(n * size, size)
        loads.append(pltpu.make_async_copy(x_hbm.at[at], held.at[at], in_sem.at[n]))
        stores.append(pltpu.make_async_copy(scaled.at[at], out_hbm.at[at], out_sem.at[n]))
    for load in loads:
        load.start()
    weights[...] = info[:layers, :slots]
    factor = info[layers:layers + 1, :]
    for n in range(blocks):
        at = pl.ds(n * size, size)
        loads[n].wait()
        scaled[at, :] = held[at, :] * factor
        stores[n].start()
    for store in stores:
        store.wait()


def on_device(initial_state, gate_angles, damp_qubits, kraus_branch, damping):
    local_amps = initial_state.shape[1]
    local_bits = local_amps.bit_length() - 1
    hi, lo = lax.axis_size("hi"), lax.axis_size("lo")
    lo_bits, hi_bits = lo.bit_length() - 1, hi.bit_length() - 1
    bits = list(range(lo_bits + hi_bits))
    rows = local_amps >> LANE_BITS
    pieces = 16
    piece_rows = rows // pieces
    orders, events = plan(bits, [b for b in (1, 2) if b in bits], pieces)
    layers, slots = damp_qubits.shape
    cfg = dict(
        parts=2, batch=8,
        lo_bits=lo_bits, bits=bits, tiles=rows // 8, pieces=pieces, piece_rows=piece_rows,
        local_bits=local_bits, layers=layers, slots=slots, orders=orders, events=events,
        whole=float(local_amps * hi * lo),
    )
    x = initial_state.reshape(2, rows, 128).transpose(1, 0, 2).reshape(2 * rows, 128)
    count = len(bits)
    stat_rows = -(-(layers * slots + 1) // 8) * 8
    vmem = pl.BlockSpec(memory_space=pltpu.VMEM)
    whole = pl.BlockSpec(memory_space=pl.ANY)
    smem = pl.BlockSpec(memory_space=pltpu.SMEM)
    out, info = pl.pallas_call(
        functools.partial(kernel, cfg),
        out_shape=(
            jax.ShapeDtypeStruct((2 * rows, 128), jnp.float32),
            jax.ShapeDtypeStruct((stat_rows, 128), jnp.float32),
        ),
        in_specs=[vmem, smem, smem, smem, whole],
        out_specs=(whole, vmem),
        scratch_shapes=[
            pltpu.VMEM((2 * rows + 8, 128), jnp.float32),
            pltpu.VMEM((2 * rows + 8, 128), jnp.float32),
            pltpu.VMEM((2, rows // 8, 8, 128), jnp.float32),
            pltpu.VMEM((2, rows // 8, 8, 128), jnp.float32),
            pltpu.VMEM((rows // 128, 2, 128, 128), jnp.float32),
            pltpu.VMEM((count, pieces, 2, piece_rows, 128), jnp.float32),
            pltpu.VMEM((count, pieces, 2, piece_rows, 128), jnp.float32),
            pltpu.VMEM((4, 256, 256), jnp.bfloat16),
            pltpu.VMEM((count + 1, stat_rows, 128), jnp.float32),
            pltpu.VMEM((count, stat_rows, 128), jnp.float32),
            pltpu.SemaphoreType.DMA((count, pieces)),
            pltpu.SemaphoreType.DMA((count, pieces)),
            pltpu.SemaphoreType.DMA((count,)),
            pltpu.SemaphoreType.DMA((count,)),
            pltpu.SemaphoreType.DMA,
            pltpu.SemaphoreType.DMA((pieces,)),
            pltpu.VMEM((8 * layers, 128), jnp.float32),
            pltpu.SMEM((8 * layers, 128), jnp.float32),
            pltpu.SemaphoreType.DMA,
        ],
        compiler_params=pltpu.CompilerParams(
            collective_id=0, has_side_effects=True, vmem_limit_bytes=56 * 1024 * 1024
        ),
    )(gate_angles.transpose(1, 0, 2), damp_qubits, kraus_branch, damping, x)
    blocks = 8
    amplitudes, weights = pl.pallas_call(
        functools.partial(scale_kernel, blocks),
        out_shape=(
            jax.ShapeDtypeStruct((2 * rows, 128), jnp.float32),
            jax.ShapeDtypeStruct((layers, slots), jnp.float32),
        ),
        in_specs=[vmem, whole],
        out_specs=(whole, vmem),
        scratch_shapes=[
            pltpu.VMEM((2 * rows, 128), jnp.float32),
            pltpu.VMEM((2 * rows, 128), jnp.float32),
            pltpu.SemaphoreType.DMA((blocks,)),
            pltpu.SemaphoreType.DMA((blocks,)),
        ],
    )(info, out)
    amplitudes = amplitudes.reshape(rows, 2, 128).transpose(1, 0, 2).reshape(2, local_amps)
    return (amplitudes, weights)


def solution(mesh):
    in_specs = (P(None, ("hi", "lo")), P(), P(), P(), P())
    out_specs = (P(None, ("hi", "lo")), P())
    return jax.shard_map(
        on_device, mesh=mesh, in_specs=in_specs, out_specs=out_specs, check_vma=False
    )
```
